32 devices in a mesh: batch: 4 (over x, core), lat: 4 (over z), lon: 2 (over y).
Axes of the slice: x: 2, y: 2, z: 4, core: 2. Of those that a mesh axis runs over, the one named last changes fastest.
Arguments:
- tokens: bfloat16 [4, 2, 48, 48, 1024], P('batch', None, 'lat', 'lon'), may hold values from -6 to 6
- weights: bfloat16 [1024, 4096], P('batch')
- regions: int32 [2, 48, 48], P(None, 'lat', 'lon'), may hold values from 0 to 3
- offsets: int32 [2], replicated, may hold values from 1 to 11, as said below
Outputs:
- mixed: bfloat16 [4, 2, 48, 48, 1024], P('batch', None, 'lat', 'lon')
The draws below stay inside these ranges and needn't reach their ends.
Inputs may be any that keep to these rules, and one draw needn't show every extreme that they name: `offsets`: element 0 lies from 1 to 5; element 1 equals 11.
All inputs are finite; a program needn't handle non-finite values.
Results may differ from the reference program's by a relative error of at most 0.0042.
Values may be sent and summed in bfloat16 or wider, within the bound.
A program may use at most 128 MiB of HBM per device.

```python
import jax
import jax.numpy as jnp
from jax import lax

D = 1024
HEADS = 16
WLEV = 2
WLAT = 6
WLON = 12
LEV = 2
SAMPLES = 4
NLAT = 48
NLON = 48


def draw_weights(key, part):
    base = jax.random.normal(key, (D, 4 * D), jnp.float32) * D ** (-0.5)
    return base.astype(jnp.bfloat16)


def draw_offsets(key, part):
    first_key = jax.random.fold_in(key, 7)
    lat_shift = jax.random.randint(first_key, (1,), 1, WLAT)
    lon_shift = jnp.full((1,), WLON - 1, jnp.int32)
    return jnp.concatenate([lat_shift.astype(jnp.int32), lon_shift]).astype(jnp.int32)


def with_ends(entries, key, smallest, high):
    index_at = [jax.random.randint(jax.random.fold_in(key, axis), (), 0, length) for axis, length in enumerate(entries.shape)]
    longest = entries.shape.index(max(entries.shape))
    beside = index_at[:longest] + [(index_at[longest] + 1) % entries.shape[longest]] + index_at[longest + 1:]
    return entries.at[tuple(index_at)].set(smallest).at[tuple(beside)].set(high)


def block_levels(key, shape, pieces, least, high):
    factor_of = 1.0
    for position, parts in pieces:
        draws = jax.random.uniform(jax.random.fold_in(jax.random.fold_in(key, 6), position), (parts,), jnp.float32, least / len(pieces), high / len(pieces))
        factor_of = factor_of * jnp.repeat(jnp.exp(draws), shape[position] // parts).reshape((-1,) + (1,) * (len(shape) - 1 - position))
    return factor_of


def gaussian(key, shape, spread, most, shards=(), kind=jnp.bfloat16):
    result = spread * jax.random.normal(key, shape, jnp.float32)
    if shards:
        result = result * block_levels(key, shape, shards, -0.22, 0.18)
    return jnp.clip(result, -most, most).astype(kind)


def setup_inputs(seed: int = 0) -> dict:
    key_list = jax.random.split(jax.random.key(seed), 5)
    return {
        "tokens": gaussian(key_list[0], (SAMPLES, LEV, NLAT, NLON, D), 1.0, 6.0, ((0, 4), (2, 4), (3, 2))),
        "weights": draw_weights(jax.random.fold_in(key_list[4], 71), 0),
        "regions": with_ends(jax.random.randint(key_list[2], (LEV, NLAT, NLON), 0, 4), jax.random.fold_in(key_list[2], 1), 0, 3).astype(jnp.int32),
        "offsets": draw_offsets(jax.random.fold_in(key_list[4], 71), 0),
    }


def layer_norm(field):
    field = field.astype(jnp.float32)
    average = lax.optimization_barrier(jnp.mean(field, -1, keepdims=True))
    centred = field - average
    variance = lax.optimization_barrier(jnp.mean(centred * centred, -1, keepdims=True))
    return (centred * lax.rsqrt(variance + 1e-05)).astype(jnp.bfloat16)

def windows(field):
    levels, rows_lat, cols_lon, features = field.shape
    field = field.reshape(levels // WLEV, WLEV, rows_lat // WLAT, WLAT, cols_lon // WLON, WLON, features)
    field = field.transpose(0, 2, 4, 1, 3, 5, 6)
    return field.reshape(-1, WLEV * WLAT * WLON, features)

def unwindows(field, levels, rows_lat, cols_lon):
    features = field.shape[-1]
    field = field.reshape(levels // WLEV, rows_lat // WLAT, cols_lon // WLON, WLEV, WLAT, WLON, features)
    field = field.transpose(0, 3, 1, 4, 2, 5, 6)
    return field.reshape(levels, rows_lat, cols_lon, features)

def attend(normed, all_weights, regions):
    levels, rows_lat, cols_lon, width = normed.shape
    qkv = jnp.dot(normed.reshape(-1, width), all_weights[:, :3 * width], preferred_element_type=jnp.float32).astype(jnp.bfloat16)
    qkv = windows(qkv.reshape(levels, rows_lat, cols_lon, 3 * width))
    num_windows, win_size = (qkv.shape[0], qkv.shape[1])
    head_size = width // HEADS
    queries = qkv[..., :width].reshape(num_windows, win_size, HEADS, head_size).astype(jnp.float32)
    keys_all = qkv[..., width:2 * width].reshape(num_windows, win_size, HEADS, head_size).astype(jnp.float32)
    values_all = qkv[..., 2 * width:].reshape(num_windows, win_size, HEADS, head_size).astype(jnp.float32)
    scores = jnp.einsum('wqhe,wkhe->whqk', queries, keys_all) * head_size ** (-0.5)
    region_ids = windows(regions[..., None])[..., 0]
    allowed = region_ids[:, None, :, None] == region_ids[:, None, None, :]
    scores = jnp.where(allowed, scores, -1e+30)
    largest = lax.optimization_barrier(jnp.max(scores, -1, keepdims=True))
    expsc = jnp.exp(scores - largest)
    attn_probs = (expsc / lax.optimization_barrier(jnp.sum(expsc, -1, keepdims=True))).astype(jnp.bfloat16)
    mixed_out = jnp.einsum('whqk,wkhe->wqhe', attn_probs.astype(jnp.float32), values_all)
    mixed_out = mixed_out.astype(jnp.bfloat16).reshape(num_windows, win_size, width)
    return unwindows(mixed_out, levels, rows_lat, cols_lon)

def reference(tokens, weights, regions, offsets):

    def per_sample(sample):
        rolled = jnp.roll(sample, (-offsets[0], -offsets[1]), axis=(1, 2))
        attended = attend(layer_norm(rolled), weights, regions)
        back_rolled = jnp.roll(attended, (offsets[0], offsets[1]), axis=(1, 2))
        projected = jnp.dot(back_rolled.reshape(-1, D), weights[:, 3 * D:], preferred_element_type=jnp.float32)
        return (sample.astype(jnp.float32) + projected.reshape(sample.shape)).astype(jnp.bfloat16)
    return lax.map(per_sample, tokens)
```

```python
import functools

import jax
import jax.numpy as jnp
from jax import lax
from jax.experimental import pallas as pl
from jax.experimental.pallas import tpu as pltpu
from jax.sharding import PartitionSpec as P

HEADS = 16
WLEV = 2
WLAT = 6
WLON = 12
GROUPS = 4
HALO = WLAT - 1
MESH = pl.DeviceIdType.MESH


def normalise(x):
    average = jnp.mean(x, -1, keepdims=True)
    centred = x - average
    variance = jnp.mean(centred * centred, -1, keepdims=True)
    return centred * lax.rsqrt(variance + 1e-05)


def kernel(
    sizes,
    off_ref, tok_ref, w_ref, edge_ref, mask_ref, out_ref,
    wqkv, wout, ext, edge_ext, mask, xw, xn, qkv, ow, nat, ret, ymat,
    local_sem, w_send, w_recv, h_send, h_recv, r_send, r_recv, *parts,
):
    attn, ret_ext = parts[:GROUPS], parts[GROUPS:]
    nb, nlat, nlon = sizes
    levels, rows, cols, width = tok_ref.shape
    win = WLEV * WLAT * WLON
    gw = width // GROUPS
    depth = w_ref.shape[0]
    half = depth // 2
    chips = nb // 2
    b, lat, lon = lax.axis_index("batch"), lax.axis_index("lat"), lax.axis_index("lon")
    chip, core = b // 2, b % 2
    side = lon % 2

    def at(db=None, dlat=0, dlon=0):
        return (
            b if db is None else db,
            (lat + dlat + nlat) % nlat,
            (lon + dlon + nlon) % nlon,
        )

    partner = (chip * 2 + 1 - core, lat, lon)
    across = (b, lat, lon + 1 - 2 * side)
    far = [(((chip + k) % chips) * 2 + core, lat, lon) for k in range(1, chips)]
    greeted = [partner, across] + far + [
        at(dlat=-1), at(dlat=1), at(dlon=1), at(dlon=-1),
        at(dlat=-1, dlon=1), at(dlat=1, dlon=-1),
    ]

    def chunk(g):
        return wqkv.at[g] if g < GROUPS else wout

    def own_loads(g):
        rows_here = pl.ds(pl.multiple_of(b * depth, depth), depth)
        if g == GROUPS:
            return [pltpu.make_async_copy(
                w_ref.at[:, pl.ds(3 * width, width)], wout.at[rows_here], local_sem.at[3 * g])]
        return [
            pltpu.make_async_copy(
                w_ref.at[:, pl.ds(t * width + g * gw, gw)],
                wqkv.at[g, rows_here, pl.ds(t * gw, gw)],
                local_sem.at[3 * g + t],
            )
            for t in range(3)
        ]

    loads = [own_loads(g) for g in range(GROUPS + 1)]
    for group in loads:
        for c in group:
            c.start()
    tok_load = pltpu.make_async_copy(tok_ref, ext.at[:, 0:rows], local_sem.at[3 * GROUPS + 1])
    edge_load_sem = local_sem.at[3 * GROUPS + 2]
    tok_load.start()
    mask_load = pltpu.make_async_copy(mask_ref.at[0], mask.at[1], edge_load_sem)
    mask_load.start()

    barrier = pltpu.get_barrier_semaphore()
    for device in greeted:
        pl.semaphore_signal(barrier, inc=1, device_id=device, device_id_type=MESH)
    pl.semaphore_wait(barrier, len(greeted))

    def send(src, dst, ssem, rsem, device):
        c = pltpu.make_async_remote_copy(
            src_ref=src, dst_ref=dst, send_sem=ssem, recv_sem=rsem,
            device_id=device, device_id_type=MESH,
        )
        c.start()
        return c

    def piece(g, owner, part):
        return chunk(g).at[pl.ds(pl.multiple_of(owner * depth + part * half, half), half)]

    nsem = 1 + 4 * (chips - 1)
    sent = []

    def send_w(g, slot, ref, device):
        i = g * nsem + slot
        c = send(ref, ref, w_send.at[i], w_recv.at[i], device)
        sent.append(c)
        return c

    xs = {}
    halos = []
    core_copies = {g: [] for g in range(GROUPS + 1)}
    ys = {}

    def first(g):
        for c in loads[g]:
            c.wait()
        for k in range(1, chips):
            xs[g, k] = send_w(g, 4 * k - 3, piece(g, b, side), far[k - 1])
        mine = chunk(g).at[pl.ds(pl.multiple_of(b * depth, depth), depth)]
        core_copies[g].append(send_w(g, 0, mine, partner))

    def origin(k):
        return ((chip + chips - k) % chips) * 2 + core

    def relay(g):
        for k in range(1, chips):
            xs[g, k].wait_recv()
            got = piece(g, origin(k), side)
            ys[g, k] = send_w(g, 4 * k - 2, got, across)
            core_copies[g].append(send_w(g, 4 * k - 1, got, partner))

    def finish(g):
        for k in range(1, chips):
            ys[g, k].wait_recv()
            core_copies[g].append(send_w(g, 4 * k, piece(g, origin(k), 1 - side), partner))
        for c in core_copies[g]:
            c.wait_recv()

    first(0)
    halos.append(send(edge_ref, edge_ext.at[:, 0:rows], h_send.at[0], h_recv.at[0], at(dlon=1)))
    halos.append(send(edge_ref, edge_ext.at[:, rows:2 * rows], h_send.at[1], h_recv.at[1], at(dlat=-1, dlon=1)))
    halos.append(send(tok_ref.at[:, 0:HALO], ext.at[:, rows:rows + HALO], h_send.at[2], h_recv.at[2], at(dlat=-1)))
    halos.append(send(mask_ref.at[1], mask.at[0], h_send.at[3], h_recv.at[3], at(dlon=1)))
    for g in range(1, GROUPS + 1):
        first(g)

    shift = off_ref[0]
    relay(0)
    tok_load.wait()
    mask_load.wait()
    for c in halos:
        c.wait_recv()
    for l in range(levels):
        for i in range(rows):
            x = normalise(ext[l, i + shift].astype(jnp.float32))
            e = normalise(edge_ext[l, i + shift])
            base = (i // WLAT) * 2 * win + l * WLAT * WLON + (i % WLAT) * WLON
            xw[base:base + 1, :] = e
            xw[base + 1:base + WLON, :] = x[0:WLON - 1]
            xw[base + win:base + win + WLON, :] = x[WLON - 1:2 * WLON - 1]
    nwin = (rows // WLAT) * (cols // WLON)
    for w in range(nwin):
        xn[w * win:(w + 1) * win, :] = xw[w * win:(w + 1) * win, :].astype(jnp.bfloat16)

    lane = lax.broadcasted_iota(jnp.int32, (win, 128), 1)
    ones = jnp.ones((win, 128), jnp.bfloat16)
    hs = width // HEADS

    def attention(g):
        for t in range(3):
            part = jnp.dot(
                xn[...], wqkv[g, :, t * gw:(t + 1) * gw], preferred_element_type=jnp.float32
            ).astype(jnp.bfloat16)
            for w in range(nwin):
                qkv[w, :, t * gw:(t + 1) * gw] = part[w * win:(w + 1) * win]

        def window(w, carry):
            allowed = mask[w % 2, w // 2].astype(jnp.float32) > 0.5
            for pair in range(gw // 128):
                q = qkv[w, :, pair * 128:(pair + 1) * 128]
                k = qkv[w, :, gw + pair * 128:gw + (pair + 1) * 128]
                v = qkv[w, :, 2 * gw + pair * 128:2 * gw + (pair + 1) * 128]
                vones = jnp.concatenate([v, ones], axis=1)
                outs = []
                for h in range(128 // hs):
                    keep = (lane // hs == h).astype(jnp.float32) * (hs ** -0.5)
                    qh = (q.astype(jnp.float32) * keep).astype(jnp.bfloat16)
                    s = lax.dot_general(
                        qh, k, (((1,), (1,)), ((), ())), preferred_element_type=jnp.float32
                    )
                    s = jnp.where(allowed, s, -1e30)
                    e = jnp.exp(s - jnp.max(s, -1, keepdims=True)).astype(jnp.bfloat16)
                    o = jnp.dot(e, vones, preferred_element_type=jnp.float32)
                    outs.append(o[:, :128] / o[:, 128:])
                ow[w, :, pair * 128:(pair + 1) * 128] = jnp.where(lane < hs, outs[0], outs[1])
            return carry

        lax.fori_loop(0, nwin, window, 0)
        gs = slice(g * gw, (g + 1) * gw)
        for l in range(levels):
            for i in range(rows):
                r = l * WLAT * WLON + (i % WLAT) * WLON
                w = (i // WLAT) * 2
                ret[g, l, i] = ow[w, r:r + 1, :].astype(jnp.bfloat16).astype(jnp.float32)
                nat[l, i, 0:WLON - 1, :] = ow[w, r + 1:r + WLON, :]
                nat[l, i, WLON - 1:2 * WLON - 1, :] = ow[w + 1, r:r + WLON, :]
                attn[g][l, HALO + i] = nat[l, i].astype(jnp.bfloat16)
        back = [
            send(attn[g].at[:, rows:rows + HALO], attn[g].at[:, 0:HALO],
                 r_send.at[3 * g], r_recv.at[3 * g], at(dlat=1)),
            send(ret.at[g], ret_ext[g].at[:, rows:2 * rows],
                 r_send.at[3 * g + 1], r_recv.at[3 * g + 1], at(dlon=-1)),
            send(ret.at[g], ret_ext[g].at[:, 0:rows],
                 r_send.at[3 * g + 2], r_recv.at[3 * g + 2], at(dlat=1, dlon=-1)),
        ]
        return back

    nat[:, :, cols - 1:cols, :] = jnp.zeros((levels, rows, 1, gw), jnp.float32)
    row_id = lax.broadcasted_iota(jnp.int32, (cols, gw), 0)
    backs = []

    def gather(g):
        for c in backs[g]:
            c.wait_recv()
        for l in range(levels):
            for i in range(rows):
                a = attn[g][l, HALO + i - shift].astype(jnp.float32)
                e = ret_ext[g][l, rows + i - shift]
                r = (l * rows + i) * cols
                ymat[r:r + cols, g * gw:(g + 1) * gw] = jnp.where(row_id == cols - 1, e, a)

    for g in range(GROUPS):
        relay(g + 1)
        finish(g)
        backs.append(attention(g))
        if g > 0:
            gather(g - 1)
    finish(GROUPS)
    gather(GROUPS - 1)

    for l in range(levels):
        for j in range(rows // WLAT):
            r = (l * rows + j * WLAT) * cols
            y = ymat[r:r + WLAT * cols, :].astype(jnp.bfloat16)
            p = jnp.dot(y, wout[...], preferred_element_type=jnp.float32)
            here = slice(j * WLAT, (j + 1) * WLAT)
            t = ext[l, here].astype(jnp.float32)
            out_ref[l, here] = (t + p.reshape(t.shape)).astype(jnp.bfloat16)

    for c in sent + halos + sum(backs, []):
        c.wait_send()


def window_ids(regions):
    levels, rows, cols = regions.shape
    field = regions.reshape(levels, rows // WLAT, WLAT, cols // WLON, WLON)
    return field.transpose(3, 1, 0, 2, 4).reshape(cols // WLON, rows // WLAT, -1)


def local(sizes, tokens, weights, regions, offsets):
    block = tokens[0]
    levels, rows, cols, width = block.shape
    win = WLEV * WLAT * WLON
    nwin = (rows // WLAT) * (cols // WLON)
    gw = width // GROUPS
    edge = block[:, :, cols - 1:, :].astype(jnp.float32)
    ids = window_ids(regions)
    mask = (ids[..., :, None] == ids[..., None, :]).astype(jnp.bfloat16)
    nw = (GROUPS + 1) * (1 + 4 * (sizes[0] // 2 - 1))
    bf, f32 = jnp.bfloat16, jnp.float32
    dma = pltpu.SemaphoreType.DMA
    anywhere = pl.BlockSpec(memory_space=pl.ANY)
    out = pl.pallas_call(
        functools.partial(kernel, sizes),
        out_shape=jax.ShapeDtypeStruct(block.shape, bf),
        in_specs=[pl.BlockSpec(memory_space=pltpu.SMEM)] + [anywhere] * 4,
        out_specs=pl.BlockSpec(memory_space=pltpu.VMEM),
        scratch_shapes=[
            pltpu.VMEM((GROUPS, width, 3 * gw), bf),
            pltpu.VMEM((width, width), bf),
            pltpu.VMEM((levels, rows + HALO, cols, width), bf),
            pltpu.VMEM((levels, 2 * rows, 1, width), f32),
            pltpu.VMEM((2, rows // WLAT, win, win), bf),
            pltpu.VMEM((nwin * win, width), f32),
            pltpu.VMEM((nwin * win, width), bf),
            pltpu.VMEM((nwin, win, 3 * gw), bf),
            pltpu.VMEM((nwin, win, gw), f32),
            pltpu.VMEM((levels, rows, cols, gw), f32),
            pltpu.VMEM((GROUPS, levels, rows, 1, gw), f32),
            pltpu.VMEM((levels * rows * cols, width), f32),
            dma((3 * GROUPS + 3,)),
            dma((nw,)),
            dma((nw,)),
            dma((4,)),
            dma((4,)),
            dma((3 * GROUPS,)),
            dma((3 * GROUPS,)),
        ]
        + [pltpu.VMEM((levels, rows + HALO, cols, gw), bf)] * GROUPS
        + [pltpu.VMEM((levels, 2 * rows, 1, gw), f32)] * GROUPS,
        compiler_params=pltpu.CompilerParams(
            collective_id=0, has_side_effects=True, vmem_limit_bytes=56 * 1024 * 1024
        ),
    )(offsets, block, weights, edge, mask)
    return out[None]


def solution(mesh):
    sizes = (mesh.shape["batch"], mesh.shape["lat"], mesh.shape["lon"])
    in_specs = (P("batch", None, "lat", "lon", None), P("batch", None), P(None, "lat", "lon"), P())
    out_specs = P("batch", None, "lat", "lon", None)
    return jax.shard_map(
        functools.partial(local, sizes), mesh=mesh, in_specs=in_specs, out_specs=out_specs, check_vma=False
    )
```

```python
import functools

import jax
import jax.numpy as jnp
from jax import lax
from jax.experimental import pallas as pl
from jax.experimental.pallas import tpu as pltpu
from jax.sharding import PartitionSpec as P

HEADS = 16
WLEV = 2
WLAT = 6
WLON = 12
GROUPS = 4
HALO = WLAT - 1
OUTS = 2
MESH = pl.DeviceIdType.MESH


def normalise(x):
    average = jnp.mean(x, -1, keepdims=True)
    centred = x - average
    variance = jnp.mean(centred * centred, -1, keepdims=True)
    return centred * lax.rsqrt(variance + 1e-05)


def kernel(
    sizes,
    off_ref, tok_ref, w_ref, reg_ref, out_ref,
    wqkv, wout, own, ext, edge, edge_ext, reg_prev, ids, mask, xw, xn, qkv, ow, nat, ret, ymat,
    local_sem, w_send, w_recv, h_send, h_recv, r_send, r_recv, *parts,
):
    attn, ret_ext = parts[:GROUPS], parts[GROUPS:]
    nb, nlat, nlon = sizes
    levels, rows, cols, width = tok_ref.shape
    win = WLEV * WLAT * WLON
    gw = width // GROUPS
    depth = w_ref.shape[0]
    half = depth // 2
    owid = width // OUTS
    chunks = GROUPS + OUTS
    chips = nb // 2
    b, lat, lon = lax.axis_index("batch"), lax.axis_index("lat"), lax.axis_index("lon")
    chip, core = b // 2, b % 2
    side = lon % 2

    def at(db=None, dlat=0, dlon=0):
        return (
            b if db is None else db,
            (lat + dlat + nlat) % nlat,
            (lon + dlon + nlon) % nlon,
        )

    partner = (chip * 2 + 1 - core, lat, lon)
    across = (b, lat, lon + 1 - 2 * side)
    far = [(((chip + k) % chips) * 2 + core, lat, lon) for k in range(1, chips)]
    greeted = [partner, across] + far + [
        at(dlat=-1), at(dlat=1), at(dlon=1), at(dlon=-1),
        at(dlat=-1, dlon=1), at(dlat=1, dlon=-1),
    ]

    def chunk(g):
        return wqkv.at[g] if g < GROUPS else wout.at[g - GROUPS]

    def own_loads(g):
        rows_here = pl.ds(pl.multiple_of(b * depth, depth), depth)
        if g >= GROUPS:
            return [pltpu.make_async_copy(
                w_ref.at[:, pl.ds(3 * width + (g - GROUPS) * owid, owid)],
                wout.at[g - GROUPS, rows_here],
                local_sem.at[2 * GROUPS + g])]
        return [
            pltpu.make_async_copy(
                w_ref.at[:, pl.ds(t * width + g * gw, gw)],
                wqkv.at[g, rows_here, pl.ds(t * gw, gw)],
                local_sem.at[3 * g + t],
            )
            for t in range(3)
        ]

    loads = [own_loads(g) for g in range(chunks)]
    for group in loads:
        for c in group:
            c.start()
    tok_load = pltpu.make_async_copy(tok_ref, own, local_sem.at[3 * GROUPS + OUTS])
    low_load = pltpu.make_async_copy(
        tok_ref.at[:, WLAT:rows], ext.at[:, 0:rows - WLAT], local_sem.at[3 * GROUPS + OUTS + 1])
    tok_load.start()
    low_load.start()

    barrier = pltpu.get_barrier_semaphore()
    for device in greeted:
        pl.semaphore_signal(barrier, inc=1, device_id=device, device_id_type=MESH)
    pl.semaphore_wait(barrier, len(greeted))

    def send(src, dst, ssem, rsem, device):
        c = pltpu.make_async_remote_copy(
            src_ref=src, dst_ref=dst, send_sem=ssem, recv_sem=rsem,
            device_id=device, device_id_type=MESH,
        )
        c.start()
        return c

    def piece(g, owner, part):
        return chunk(g).at[pl.ds(pl.multiple_of(owner * depth + part * half, half), half)]

    nsem = 1 + 4 * (chips - 1)
    sent = []

    def send_w(g, slot, ref, device):
        i = g * nsem + slot
        c = send(ref, ref, w_send.at[i], w_recv.at[i], device)
        sent.append(c)
        return c

    xs = {}
    halos = []
    core_copies = {g: [] for g in range(chunks)}
    ys = {}

    def first(g):
        for c in loads[g]:
            c.wait()
        for k in range(1, chips):
            xs[g, k] = send_w(g, 4 * k - 3, piece(g, b, side), far[k - 1])
        mine = chunk(g).at[pl.ds(pl.multiple_of(b * depth, depth), depth)]
        core_copies[g].append(send_w(g, 0, mine, partner))

    def origin(k):
        return ((chip + chips - k) % chips) * 2 + core

    def relay(g):
        for k in range(1, chips):
            xs[g, k].wait_recv()
            got = piece(g, origin(k), side)
            ys[g, k] = send_w(g, 4 * k - 2, got, across)
            core_copies[g].append(send_w(g, 4 * k - 1, got, partner))

    def finish(g):
        for k in range(1, chips):
            ys[g, k].wait_recv()
            core_copies[g].append(send_w(g, 4 * k, piece(g, origin(k), 1 - side), partner))
        for c in core_copies[g]:
            c.wait_recv()

    lat_halo = send(tok_ref.at[:, 0:HALO], ext.at[:, rows - WLAT:rows - WLAT + HALO],
                    h_send.at[0], h_recv.at[0], at(dlat=-1))
    reg_halo = send(reg_ref, reg_prev, h_send.at[1], h_recv.at[1], at(dlon=1))
    for g in range(chunks):
        first(g)

    shift = off_ref[0]
    tok_load.wait()
    for l in range(levels):
        for i in range(rows):
            edge[l, i] = own[l, i].astype(jnp.float32)[cols - 1:cols]
    near_halo = send(edge, edge_ext.at[:, 0:rows], h_send.at[2], h_recv.at[2], at(dlon=1))
    diag_halo = send(edge, edge_ext.at[:, rows:2 * rows], h_send.at[3], h_recv.at[3], at(dlat=-1, dlon=1))
    halos = [lat_halo, reg_halo, near_halo, diag_halo]

    def masks(ref, k):
        for i in range(rows):
            ids[i * levels:(i + 1) * levels, :] = ref[i].astype(jnp.float32)
        table = ids[...].astype(jnp.bfloat16)
        pos = lax.broadcasted_iota(jnp.int32, (levels * rows, win), 1)
        which = lax.broadcasted_iota(jnp.int32, (levels * rows, win), 0)
        pos_t = lax.broadcasted_iota(jnp.int32, (win, levels * rows), 0)
        which_t = lax.broadcasted_iota(jnp.int32, (win, levels * rows), 1)
        col = (lax.broadcasted_iota(jnp.int32, (cols, win), 0)
               == k * WLON + lax.broadcasted_iota(jnp.int32, (cols, win), 1) % WLON)
        col_t = (lax.broadcasted_iota(jnp.int32, (win, cols), 1)
                 == k * WLON + lax.broadcasted_iota(jnp.int32, (win, cols), 0) % WLON)
        wide = jnp.dot(table, col.astype(jnp.float32).astype(jnp.bfloat16), preferred_element_type=jnp.float32)
        tall = lax.dot_general(
            col_t.astype(jnp.float32).astype(jnp.bfloat16), table, (((1,), (1,)), ((), ())),
            preferred_element_type=jnp.float32)

        def row_of(p, lw):
            return (lw * WLAT + p % (WLAT * WLON) // WLON) * levels + p // (WLAT * WLON)

        for lw in range(rows // WLAT):
            r = jnp.sum(jnp.where(which == row_of(pos, lw), wide, 0.0), 0, keepdims=True)
            c = jnp.sum(jnp.where(which_t == row_of(pos_t, lw), tall, 0.0), 1, keepdims=True)
            mask[lw * 2 + 1 - k] = (r == c).astype(jnp.float32)

    def norm(lw):
        src = own if lw == 0 else ext
        for l in range(levels):
            for ii in range(WLAT):
                x = normalise(src[l, ii + shift].astype(jnp.float32))
                e = normalise(edge_ext[l, lw * WLAT + ii + shift])
                base = lw * 2 * win + l * WLAT * WLON + ii * WLON
                xw[base:base + 1, :] = e
                xw[base + 1:base + WLON, :] = x[0:WLON - 1]
                xw[base + win:base + win + WLON, :] = x[WLON - 1:2 * WLON - 1]
        for w in range(2 * lw, 2 * lw + 2):
            xn[w * win:(w + 1) * win, :] = xw[w * win:(w + 1) * win, :].astype(jnp.bfloat16)

    masks(reg_ref, 0)
    relay(0)
    reg_halo.wait_recv()
    masks(reg_prev, 1)
    near_halo.wait_recv()
    diag_halo.wait_recv()
    norm(0)
    relay(1)
    nwin = (rows // WLAT) * (cols // WLON)
    for w in range(nwin):
        xn[w * win:(w + 1) * win, :] = xw[w * win:(w + 1) * win, :].astype(jnp.bfloat16)

    lane = lax.broadcasted_iota(jnp.int32, (win, 128), 1)
    ones = jnp.ones((win, 128), jnp.bfloat16)
    hs = width // HEADS

    def attention(g, lw):
        both = slice(lw * 2 * win, (lw + 1) * 2 * win)
        for t in range(3):
            part = jnp.dot(
                xn[both, :], wqkv[g, :, t * gw:(t + 1) * gw], preferred_element_type=jnp.float32
            ).astype(jnp.bfloat16)
            for w in range(2):
                qkv[w, :, t * gw:(t + 1) * gw] = part[w * win:(w + 1) * win]

        def window(w, carry):
            allowed = mask[lw * 2 + w] > 0.5
            for pair in range(gw // 128):
                q = qkv[w, :, pair * 128:(pair + 1) * 128]
                k = qkv[w, :, gw + pair * 128:gw + (pair + 1) * 128]
                v = qkv[w, :, 2 * gw + pair * 128:2 * gw + (pair + 1) * 128]
                vones = jnp.concatenate([v, ones], axis=1)
                outs = []
                for h in range(128 // hs):
                    keep = (lane // hs == h).astype(jnp.float32) * (hs ** -0.5)
                    qh = (q.astype(jnp.float32) * keep).astype(jnp.bfloat16)
                    s = lax.dot_general(
                        qh, k, (((1,), (1,)), ((), ())), preferred_element_type=jnp.float32
                    )
                    s = jnp.where(allowed, s, -1e30)
                    e = jnp.exp(s - jnp.max(s, -1, keepdims=True)).astype(jnp.bfloat16)
                    o = jnp.dot(e, vones, preferred_element_type=jnp.float32)
                    outs.append(o[:, :128] / o[:, 128:])
                ow[w, :, pair * 128:(pair + 1) * 128] = jnp.where(lane < hs, outs[0], outs[1])
            return carry

        lax.fori_loop(0, 2, window, 0)
        for l in range(levels):
            for ii in range(WLAT):
                i = lw * WLAT + ii
                r = l * WLAT * WLON + ii * WLON
                w = 0
                ret[g, l, i] = ow[w, r:r + 1, :].astype(jnp.bfloat16).astype(jnp.float32)
                nat[l, i, 0:WLON - 1, :] = ow[w, r + 1:r + WLON, :]
                nat[l, i, WLON - 1:2 * WLON - 1, :] = ow[w + 1, r:r + WLON, :]
                attn[g][l, HALO + i] = nat[l, i].astype(jnp.bfloat16)
    def give(g):
        return [
            send(attn[g].at[:, rows:rows + HALO], attn[g].at[:, 0:HALO],
                 r_send.at[3 * g], r_recv.at[3 * g], at(dlat=1)),
            send(ret.at[g], ret_ext[g].at[:, rows:2 * rows],
                 r_send.at[3 * g + 1], r_recv.at[3 * g + 1], at(dlon=-1)),
            send(ret.at[g], ret_ext[g].at[:, 0:rows],
                 r_send.at[3 * g + 2], r_recv.at[3 * g + 2], at(dlat=1, dlon=-1)),
        ]

    nat[:, :, cols - 1:cols, :] = jnp.zeros((levels, rows, 1, gw), jnp.float32)
    row_id = lax.broadcasted_iota(jnp.int32, (cols, gw), 0)
    backs = []

    def gather(g):
        for c in backs[g]:
            c.wait_recv()
        for l in range(levels):
            for i in range(rows):
                a = attn[g][l, HALO + i - shift].astype(jnp.float32)
                e = ret_ext[g][l, rows + i - shift]
                r = (l * rows + i) * cols
                ymat[r:r + cols, g * gw:(g + 1) * gw] = jnp.where(row_id == cols - 1, e, a)

    finish(0)
    attention(0, 0)
    low_load.wait()
    lat_halo.wait_recv()
    norm(1)
    for g in range(GROUPS):
        if g > 0:
            finish(g)
            attention(g, 0)
        attention(g, 1)
        backs.append(give(g))
        relay(g + 2)
        if g > 0:
            gather(g - 1)
    finish(GROUPS)
    finish(GROUPS + 1)
    gather(GROUPS - 1)

    for l in range(levels):
        for j in range(rows // WLAT):
            r = (l * rows + j * WLAT) * cols
            y = ymat[r:r + WLAT * cols, :].astype(jnp.bfloat16)
            here = slice(j * WLAT, (j + 1) * WLAT)
            for n in range(OUTS):
                side_cols = slice(n * owid, (n + 1) * owid)
                p = jnp.dot(y, wout[n], preferred_element_type=jnp.float32)
                t = own[l, here, :, side_cols].astype(jnp.float32)
                out_ref[l, here, :, side_cols] = (t + p.reshape(t.shape)).astype(jnp.bfloat16)

    for c in sent + halos + sum(backs, []):
        c.wait_send()


def local(sizes, tokens, weights, regions, offsets):
    block = tokens[0]
    levels, rows, cols, width = block.shape
    win = WLEV * WLAT * WLON
    nwin = (rows // WLAT) * (cols // WLON)
    gw = width // GROUPS
    nw = (GROUPS + OUTS) * (1 + 4 * (sizes[0] // 2 - 1))
    bf, f32 = jnp.bfloat16, jnp.float32
    dma = pltpu.SemaphoreType.DMA
    anywhere = pl.BlockSpec(memory_space=pl.ANY)
    out = pl.pallas_call(
        functools.partial(kernel, sizes),
        out_shape=jax.ShapeDtypeStruct(block.shape, bf),
        in_specs=[pl.BlockSpec(memory_space=pltpu.SMEM), anywhere, anywhere, pl.BlockSpec(memory_space=pltpu.VMEM)],
        out_specs=pl.BlockSpec(memory_space=pltpu.VMEM),
        scratch_shapes=[
            pltpu.VMEM((GROUPS, width, 3 * gw), bf),
            pltpu.VMEM((OUTS, width, width // OUTS), bf),
            pltpu.VMEM((levels, rows, cols, width), bf),
            pltpu.VMEM((levels, rows - WLAT + HALO, cols, width), bf),
            pltpu.VMEM((levels, rows, 1, width), f32),
            pltpu.VMEM((levels, 2 * rows, 1, width), f32),
            pltpu.VMEM((rows, levels, cols), jnp.int32),
            pltpu.VMEM((levels * rows, cols), f32),
            pltpu.VMEM((nwin, win, win), f32),
            pltpu.VMEM((nwin * win, width), f32),
            pltpu.VMEM((nwin * win, width), bf),
            pltpu.VMEM((2, win, 3 * gw), bf),
            pltpu.VMEM((2, win, gw), f32),
            pltpu.VMEM((levels, rows, cols, gw), f32),
            pltpu.VMEM((GROUPS, levels, rows, 1, gw), f32),
            pltpu.VMEM((levels * rows * cols, width), f32),
            dma((3 * GROUPS + OUTS + 2,)),
            dma((nw,)),
            dma((nw,)),
            dma((4,)),
            dma((4,)),
            dma((3 * GROUPS,)),
            dma((3 * GROUPS,)),
        ]
        + [pltpu.VMEM((levels, rows + HALO, cols, gw), bf)] * GROUPS
        + [pltpu.VMEM((levels, 2 * rows, 1, gw), f32)] * GROUPS,
        compiler_params=pltpu.CompilerParams(
            collective_id=0, has_side_effects=True, vmem_limit_bytes=56 * 1024 * 1024
        ),
    )(offsets, block, weights, regions.transpose(1, 0, 2))
    return out[None]


def solution(mesh):
    sizes = (mesh.shape["batch"], mesh.shape["lat"], mesh.shape["lon"])
    in_specs = (P("batch", None, "lat", "lon", None), P("batch", None), P(None, "lat", "lon"), P())
    out_specs = P("batch", None, "lat", "lon", None)
    return jax.shard_map(
        functools.partial(local, sizes), mesh=mesh, in_specs=in_specs, out_specs=out_specs, check_vma=False
    )
```

```python
import functools

import jax
import jax.numpy as jnp
from jax import lax
from jax.experimental import pallas as pl
from jax.experimental.pallas import tpu as pltpu
from jax.sharding import PartitionSpec as P

HEADS = 16
WLEV = 2
WLAT = 6
WLON = 12
GROUPS = 4
HALO = WLAT - 1
OUTS = 2
MESH = pl.DeviceIdType.MESH


def normalise(x):
    average = jnp.mean(x, -1, keepdims=True)
    centred = x - average
    variance = jnp.mean(centred * centred, -1, keepdims=True)
    return centred * lax.rsqrt(variance + 1e-05)


def kernel(
    sizes,
    off_ref, tok_ref, w_ref, reg_ref, out_ref,
    wqkv, wout, own, ext, edge, edge_ext, reg_prev, ids, mask, xw, xn, qkv, ow, nat, ret, ymat,
    local_sem, w_send, w_recv, h_send, h_recv, r_send, r_recv, *parts,
):
    attn, ret_ext = parts[:GROUPS], parts[GROUPS:]
    nb, nlat, nlon = sizes
    levels, rows, cols, width = tok_ref.shape
    win = WLEV * WLAT * WLON
    gw = width // GROUPS
    depth = w_ref.shape[0]
    half = depth // 2
    owid = width // OUTS
    chunks = GROUPS + OUTS
    chips = nb // 2
    b, lat, lon = lax.axis_index("batch"), lax.axis_index("lat"), lax.axis_index("lon")
    chip, core = b // 2, b % 2
    side = lon % 2

    def at(db=None, dlat=0, dlon=0):
        return (
            b if db is None else db,
            (lat + dlat + nlat) % nlat,
            (lon + dlon + nlon) % nlon,
        )

    partner = (chip * 2 + 1 - core, lat, lon)
    across = (b, lat, lon + 1 - 2 * side)
    far = [(((chip + k) % chips) * 2 + core, lat, lon) for k in range(1, chips)]
    greeted = [partner, across] + far + [
        at(dlat=-1), at(dlat=1), at(dlon=1), at(dlon=-1),
        at(dlat=-1, dlon=1), at(dlat=1, dlon=-1),
    ]

    def chunk(g):
        return wqkv.at[g] if g < GROUPS else wout.at[g - GROUPS]

    def own_loads(g):
        rows_here = pl.ds(pl.multiple_of(b * depth, depth), depth)
        if g >= GROUPS:
            return [pltpu.make_async_copy(
                w_ref.at[:, pl.ds(3 * width + (g - GROUPS) * owid, owid)],
                wout.at[g - GROUPS, rows_here],
                local_sem.at[2 * GROUPS + g])]
        return [
            pltpu.make_async_copy(
                w_ref.at[:, pl.ds(t * width + g * gw, gw)],
                wqkv.at[g, rows_here, pl.ds(t * gw, gw)],
                local_sem.at[3 * g + t],
            )
            for t in range(3)
        ]

    loads = [own_loads(g) for g in range(chunks)]
    for group in loads:
        for c in group:
            c.start()
    tok_load = pltpu.make_async_copy(tok_ref, own, local_sem.at[3 * GROUPS + OUTS])
    low_load = pltpu.make_async_copy(
        tok_ref.at[:, WLAT:rows], ext.at[:, 0:rows - WLAT], local_sem.at[3 * GROUPS + OUTS + 1])
    tok_load.start()
    low_load.start()

    barrier = pltpu.get_barrier_semaphore()
    for device in greeted:
        pl.semaphore_signal(barrier, inc=1, device_id=device, device_id_type=MESH)
    pl.semaphore_wait(barrier, len(greeted))

    def send(src, dst, ssem, rsem, device):
        c = pltpu.make_async_remote_copy(
            src_ref=src, dst_ref=dst, send_sem=ssem, recv_sem=rsem,
            device_id=device, device_id_type=MESH,
        )
        c.start()
        return c

    def piece(g, owner, part):
        return chunk(g).at[pl.ds(pl.multiple_of(owner * depth + part * half, half), half)]

    nsem = 1 + 4 * (chips - 1)
    sent = []

    def send_w(g, slot, ref, device):
        i = g * nsem + slot
        c = send(ref, ref, w_send.at[i], w_recv.at[i], device)
        sent.append(c)
        return c

    xs = {}
    halos = []
    core_copies = {g: [] for g in range(chunks)}
    ys = {}

    def first(g):
        for c in loads[g]:
            c.wait()
        mine = chunk(g).at[pl.ds(pl.multiple_of(b * depth, depth), depth)]
        core_copies[g].append(send_w(g, 0, mine, partner))

    def cross(g):
        for k in range(1, chips):
            xs[g, k] = send_w(g, 4 * k - 3, piece(g, b, side), far[k - 1])

    def origin(k):
        return ((chip + chips - k) % chips) * 2 + core

    def relay(g):
        for k in range(1, chips):
            xs[g, k].wait_recv()
        for ahead in ([1, 2] if g == 0 else [g + 2]):
            if ahead < chunks:
                cross(ahead)
        for k in range(1, chips):
            got = piece(g, origin(k), side)
            ys[g, k] = send_w(g, 4 * k - 2, got, across)
            core_copies[g].append(send_w(g, 4 * k - 1, got, partner))

    def finish(g):
        for k in range(1, chips):
            ys[g, k].wait_recv()
            core_copies[g].append(send_w(g, 4 * k, piece(g, origin(k), 1 - side), partner))
        for c in core_copies[g]:
            c.wait_recv()

    lat_halo = send(tok_ref.at[:, 0:HALO], ext.at[:, rows - WLAT:rows - WLAT + HALO],
                    h_send.at[0], h_recv.at[0], at(dlat=-1))
    reg_halo = send(reg_ref, reg_prev, h_send.at[1], h_recv.at[1], at(dlon=1))
    for g in range(chunks):
        first(g)
        if g == 0:
            cross(0)

    shift = off_ref[0]
    tok_load.wait()
    for l in range(levels):
        for i in range(rows):
            edge[l, i] = own[l, i].astype(jnp.float32)[cols - 1:cols]
    near_halo = send(edge, edge_ext.at[:, 0:rows], h_send.at[2], h_recv.at[2], at(dlon=1))
    diag_halo = send(edge, edge_ext.at[:, rows:2 * rows], h_send.at[3], h_recv.at[3], at(dlat=-1, dlon=1))
    halos = [lat_halo, reg_halo, near_halo, diag_halo]

    def masks(ref, k):
        for i in range(rows):
            ids[i * levels:(i + 1) * levels, :] = ref[i].astype(jnp.float32)
        table = ids[...].astype(jnp.bfloat16)
        pos = lax.broadcasted_iota(jnp.int32, (levels * rows, win), 1)
        which = lax.broadcasted_iota(jnp.int32, (levels * rows, win), 0)
        pos_t = lax.broadcasted_iota(jnp.int32, (win, levels * rows), 0)
        which_t = lax.broadcasted_iota(jnp.int32, (win, levels * rows), 1)
        col = (lax.broadcasted_iota(jnp.int32, (cols, win), 0)
               == k * WLON + lax.broadcasted_iota(jnp.int32, (cols, win), 1) % WLON)
        col_t = (lax.broadcasted_iota(jnp.int32, (win, cols), 1)
                 == k * WLON + lax.broadcasted_iota(jnp.int32, (win, cols), 0) % WLON)
        wide = jnp.dot(table, col.astype(jnp.float32).astype(jnp.bfloat16), preferred_element_type=jnp.float32)
        tall = lax.dot_general(
            col_t.astype(jnp.float32).astype(jnp.bfloat16), table, (((1,), (1,)), ((), ())),
            preferred_element_type=jnp.float32)

        def row_of(p, lw):
            return (lw * WLAT + p % (WLAT * WLON) // WLON) * levels + p // (WLAT * WLON)

        for lw in range(rows // WLAT):
            r = jnp.sum(jnp.where(which == row_of(pos, lw), wide, 0.0), 0, keepdims=True)
            c = jnp.sum(jnp.where(which_t == row_of(pos_t, lw), tall, 0.0), 1, keepdims=True)
            mask[lw * 2 + 1 - k] = (r == c).astype(jnp.float32)

    def norm(lw):
        src = own if lw == 0 else ext
        for l in range(levels):
            for ii in range(WLAT):
                x = normalise(src[l, ii + shift].astype(jnp.float32))
                e = normalise(edge_ext[l, lw * WLAT + ii + shift])
                base = lw * 2 * win + l * WLAT * WLON + ii * WLON
                xw[base:base + 1, :] = e
                xw[base + 1:base + WLON, :] = x[0:WLON - 1]
                xw[base + win:base + win + WLON, :] = x[WLON - 1:2 * WLON - 1]
        for w in range(2 * lw, 2 * lw + 2):
            xn[w * win:(w + 1) * win, :] = xw[w * win:(w + 1) * win, :].astype(jnp.bfloat16)

    masks(reg_ref, 0)
    relay(0)
    reg_halo.wait_recv()
    masks(reg_prev, 1)
    near_halo.wait_recv()
    diag_halo.wait_recv()
    norm(0)
    relay(1)
    nwin = (rows // WLAT) * (cols // WLON)
    for w in range(nwin):
        xn[w * win:(w + 1) * win, :] = xw[w * win:(w + 1) * win, :].astype(jnp.bfloat16)

    lane = lax.broadcasted_iota(jnp.int32, (win, 128), 1)
    ones = jnp.ones((win, 128), jnp.bfloat16)
    hs = width // HEADS

    def attention(g, lw):
        both = slice(lw * 2 * win, (lw + 1) * 2 * win)
        for t in range(3):
            part = jnp.dot(
                xn[both, :], wqkv[g, :, t * gw:(t + 1) * gw], preferred_element_type=jnp.float32
            ).astype(jnp.bfloat16)
            for w in range(2):
                qkv[w, :, t * gw:(t + 1) * gw] = part[w * win:(w + 1) * win]

        def window(w, carry):
            allowed = mask[lw * 2 + w] > 0.5
            for pair in range(gw // 128):
                q = qkv[w, :, pair * 128:(pair + 1) * 128]
                k = qkv[w, :, gw + pair * 128:gw + (pair + 1) * 128]
                v = qkv[w, :, 2 * gw + pair * 128:2 * gw + (pair + 1) * 128]
                vones = jnp.concatenate([v, ones], axis=1)
                outs = []
                for h in range(128 // hs):
                    keep = (lane // hs == h).astype(jnp.float32) * (hs ** -0.5)
                    qh = (q.astype(jnp.float32) * keep).astype(jnp.bfloat16)
                    s = lax.dot_general(
                        qh, k, (((1,), (1,)), ((), ())), preferred_element_type=jnp.float32
                    )
                    s = jnp.where(allowed, s, -1e30)
                    e = jnp.exp(s - jnp.max(s, -1, keepdims=True)).astype(jnp.bfloat16)
                    o = jnp.dot(e, vones, preferred_element_type=jnp.float32)
                    outs.append(o[:, :128] / o[:, 128:])
                ow[w, :, pair * 128:(pair + 1) * 128] = jnp.where(lane < hs, outs[0], outs[1])
            return carry

        for w in range(2):
            window(w, 0)
        for l in range(levels):
            for ii in range(WLAT):
                i = lw * WLAT + ii
                r = l * WLAT * WLON + ii * WLON
                w = 0
                ret[g, l, i] = ow[w, r:r + 1, :].astype(jnp.bfloat16).astype(jnp.float32)
                nat[l, i, 0:WLON - 1, :] = ow[w, r + 1:r + WLON, :]
                nat[l, i, WLON - 1:2 * WLON - 1, :] = ow[w + 1, r:r + WLON, :]
                attn[g][l, HALO + i] = nat[l, i].astype(jnp.bfloat16)
    def give(g):
        return [
            send(attn[g].at[:, rows:rows + HALO], attn[g].at[:, 0:HALO],
                 r_send.at[3 * g], r_recv.at[3 * g], at(dlat=1)),
            send(ret.at[g], ret_ext[g].at[:, rows:2 * rows],
                 r_send.at[3 * g + 1], r_recv.at[3 * g + 1], at(dlon=-1)),
            send(ret.at[g], ret_ext[g].at[:, 0:rows],
                 r_send.at[3 * g + 2], r_recv.at[3 * g + 2], at(dlat=1, dlon=-1)),
        ]

    nat[:, :, cols - 1:cols, :] = jnp.zeros((levels, rows, 1, gw), jnp.float32)
    row_id = lax.broadcasted_iota(jnp.int32, (cols, gw), 0)
    backs = []

    def gather(g):
        for c in backs[g]:
            c.wait_recv()
        for l in range(levels):
            for i in range(rows):
                a = attn[g][l, HALO + i - shift].astype(jnp.float32)
                e = ret_ext[g][l, rows + i - shift]
                r = (l * rows + i) * cols
                ymat[r:r + cols, g * gw:(g + 1) * gw] = jnp.where(row_id == cols - 1, e, a)

    finish(0)
    attention(0, 0)
    low_load.wait()
    lat_halo.wait_recv()
    norm(1)
    for g in range(GROUPS):
        if g > 0:
            finish(g)
            attention(g, 0)
        relay(g + 2)
        attention(g, 1)
        backs.append(give(g))
        if g > 0:
            gather(g - 1)
    finish(GROUPS)
    finish(GROUPS + 1)
    gather(GROUPS - 1)

    for l in range(levels):
        for j in range(rows // WLAT):
            r = (l * rows + j * WLAT) * cols
            y = ymat[r:r + WLAT * cols, :].astype(jnp.bfloat16)
            here = slice(j * WLAT, (j + 1) * WLAT)
            for n in range(OUTS):
                side_cols = slice(n * owid, (n + 1) * owid)
                p = jnp.dot(y, wout[n], preferred_element_type=jnp.float32)
                t = own[l, here, :, side_cols].astype(jnp.float32)
                out_ref[l, here, :, side_cols] = (t + p.reshape(t.shape)).astype(jnp.bfloat16)

    for c in sent + halos + sum(backs, []):
        c.wait_send()


def local(sizes, tokens, weights, regions, offsets):
    block = tokens[0]
    levels, rows, cols, width = block.shape
    win = WLEV * WLAT * WLON
    nwin = (rows // WLAT) * (cols // WLON)
    gw = width // GROUPS
    nw = (GROUPS + OUTS) * (1 + 4 * (sizes[0] // 2 - 1))
    bf, f32 = jnp.bfloat16, jnp.float32
    dma = pltpu.SemaphoreType.DMA
    anywhere = pl.BlockSpec(memory_space=pl.ANY)
    out = pl.pallas_call(
        functools.partial(kernel, sizes),
        out_shape=jax.ShapeDtypeStruct(block.shape, bf),
        in_specs=[pl.BlockSpec(memory_space=pltpu.SMEM), anywhere, anywhere, pl.BlockSpec(memory_space=pltpu.VMEM)],
        out_specs=pl.BlockSpec(memory_space=pltpu.VMEM),
        scratch_shapes=[
            pltpu.VMEM((GROUPS, width, 3 * gw), bf),
            pltpu.VMEM((OUTS, width, width // OUTS), bf),
            pltpu.VMEM((levels, rows, cols, width), bf),
            pltpu.VMEM((levels, rows - WLAT + HALO, cols, width), bf),
            pltpu.VMEM((levels, rows, 1, width), f32),
            pltpu.VMEM((levels, 2 * rows, 1, width), f32),
            pltpu.VMEM((rows, levels, cols), jnp.int32),
            pltpu.VMEM((levels * rows, cols), f32),
            pltpu.VMEM((nwin, win, win), f32),
            pltpu.VMEM((nwin * win, width), f32),
            pltpu.VMEM((nwin * win, width), bf),
            pltpu.VMEM((2, win, 3 * gw), bf),
            pltpu.VMEM((2, win, gw), f32),
            pltpu.VMEM((levels, rows, cols, gw), f32),
            pltpu.VMEM((GROUPS, levels, rows, 1, gw), f32),
            pltpu.VMEM((levels * rows * cols, width), f32),
            dma((3 * GROUPS + OUTS + 2,)),
            dma((nw,)),
            dma((nw,)),
            dma((4,)),
            dma((4,)),
            dma((3 * GROUPS,)),
            dma((3 * GROUPS,)),
        ]
        + [pltpu.VMEM((levels, rows + HALO, cols, gw), bf)] * GROUPS
        + [pltpu.VMEM((levels, 2 * rows, 1, gw), f32)] * GROUPS,
        compiler_params=pltpu.CompilerParams(
            collective_id=0, has_side_effects=True, vmem_limit_bytes=56 * 1024 * 1024
        ),
    )(offsets, block, weights, regions.transpose(1, 0, 2))
    return out[None]


def solution(mesh):
    sizes = (mesh.shape["batch"], mesh.shape["lat"], mesh.shape["lon"])
    in_specs = (P("batch", None, "lat", "lon", None), P("batch", None), P(None, "lat", "lon"), P())
    out_specs = P("batch", None, "lat", "lon", None)
    return jax.shard_map(
        functools.partial(local, sizes), mesh=mesh, in_specs=in_specs, out_specs=out_specs, check_vma=False
    )
```

```python
import functools

import jax
import jax.numpy as jnp
from jax import lax
from jax.experimental import pallas as pl
from jax.experimental.pallas import tpu as pltpu
from jax.sharding import PartitionSpec as P

HEADS = 16
WLEV = 2
WLAT = 6
WLON = 12
GROUPS = 4
HALO = WLAT - 1
OUTS = 2
MESH = pl.DeviceIdType.MESH


def normalise(x):
    average = jnp.mean(x, -1, keepdims=True)
    centred = x - average
    variance = jnp.mean(centred * centred, -1, keepdims=True)
    return centred * lax.rsqrt(variance + 1e-05)


def kernel(
    sizes,
    off_ref, tok_ref, w_ref, reg_ref, out_ref,
    wqkv, wout, own, ext, edge, edge_ext, reg_prev, ids, mask, xw, xn, qkv, ow, nat, ret, ymat,
    local_sem, w_send, w_recv, h_send, h_recv, r_send, r_recv, *parts,
):
    attn, ret_ext = parts[:GROUPS], parts[GROUPS:]
    nb, nlat, nlon = sizes
    levels, rows, cols, width = tok_ref.shape
    win = WLEV * WLAT * WLON
    gw = width // GROUPS
    depth = w_ref.shape[0]
    half = depth // 2
    owid = width // OUTS
    chunks = GROUPS + OUTS
    chips = nb // 2
    b, lat, lon = lax.axis_index("batch"), lax.axis_index("lat"), lax.axis_index("lon")
    chip, core = b // 2, b % 2
    side = lon % 2

    def at(db=None, dlat=0, dlon=0):
        return (
            b if db is None else db,
            (lat + dlat + nlat) % nlat,
            (lon + dlon + nlon) % nlon,
        )

    partner = (chip * 2 + 1 - core, lat, lon)
    across = (b, lat, lon + 1 - 2 * side)
    far = [(((chip + k) % chips) * 2 + core, lat, lon) for k in range(1, chips)]
    greeted = [partner, across] + far + [
        at(dlat=-1), at(dlat=1), at(dlon=1), at(dlon=-1),
        at(dlat=-1, dlon=1), at(dlat=1, dlon=-1),
    ]

    def chunk(g):
        return wqkv.at[g] if g < GROUPS else wout.at[g - GROUPS]

    def own_loads(g):
        rows_here = pl.ds(pl.multiple_of(b * depth, depth), depth)
        if g >= GROUPS:
            return [pltpu.make_async_copy(
                w_ref.at[:, pl.ds(3 * width + (g - GROUPS) * owid, owid)],
                wout.at[g - GROUPS, rows_here],
                local_sem.at[2 * GROUPS + g])]
        return [
            pltpu.make_async_copy(
                w_ref.at[:, pl.ds(t * width + g * gw, gw)],
                wqkv.at[g, rows_here, pl.ds(t * gw, gw)],
                local_sem.at[3 * g + t],
            )
            for t in range(3)
        ]

    loads = [own_loads(g) for g in range(chunks)]
    for group in loads:
        for c in group:
            c.start()
    tok_load = pltpu.make_async_copy(tok_ref, own, local_sem.at[3 * GROUPS + OUTS])
    low_load = pltpu.make_async_copy(
        tok_ref.at[:, WLAT:rows], ext.at[:, 0:rows - WLAT], local_sem.at[3 * GROUPS + OUTS + 1])
    tok_load.start()
    low_load.start()

    barrier = pltpu.get_barrier_semaphore()
    for device in greeted:
        pl.semaphore_signal(barrier, inc=1, device_id=device, device_id_type=MESH)
    pl.semaphore_wait(barrier, len(greeted))

    def send(src, dst, ssem, rsem, device):
        c = pltpu.make_async_remote_copy(
            src_ref=src, dst_ref=dst, send_sem=ssem, recv_sem=rsem,
            device_id=device, device_id_type=MESH,
        )
        c.start()
        return c

    def piece(g, owner, part):
        return chunk(g).at[pl.ds(pl.multiple_of(owner * depth + part * half, half), half)]

    nsem = 1 + 4 * (chips - 1)
    sent = []

    def send_w(g, slot, ref, device):
        i = g * nsem + slot
        c = send(ref, ref, w_send.at[i], w_recv.at[i], device)
        sent.append(c)
        return c

    xs = {}
    halos = []
    core_copies = {g: [] for g in range(chunks)}
    ys = {}

    def first(g):
        for c in loads[g]:
            c.wait()
        mine = chunk(g).at[pl.ds(pl.multiple_of(b * depth, depth), depth)]
        core_copies[g].append(send_w(g, 0, mine, partner))

    def cross(g):
        for k in range(1, chips):
            xs[g, k] = send_w(g, 4 * k - 3, piece(g, b, side), far[k - 1])

    def origin(k):
        return ((chip + chips - k) % chips) * 2 + core

    def relay(g):
        for k in range(1, chips):
            xs[g, k].wait_recv()
        for ahead in ([1, 2] if g == 0 else [g + 2]):
            if ahead < chunks:
                cross(ahead)
        for k in range(1, chips):
            got = piece(g, origin(k), side)
            ys[g, k] = send_w(g, 4 * k - 2, got, across)
            core_copies[g].append(send_w(g, 4 * k - 1, got, partner))

    def finish(g):
        for k in range(1, chips):
            ys[g, k].wait_recv()
            core_copies[g].append(send_w(g, 4 * k, piece(g, origin(k), 1 - side), partner))
        for c in core_copies[g]:
            c.wait_recv()

    lat_halo = send(tok_ref.at[:, 0:HALO], ext.at[:, rows - WLAT:rows - WLAT + HALO],
                    h_send.at[0], h_recv.at[0], at(dlat=-1))
    reg_halo = send(reg_ref, reg_prev, h_send.at[1], h_recv.at[1], at(dlon=1))
    for g in range(chunks):
        first(g)
        if g == 0:
            cross(0)

    shift = off_ref[0]
    tok_load.wait()
    for l in range(levels):
        for i in range(rows):
            edge[l, i] = own[l, i].astype(jnp.float32)[cols - 1:cols]
    near_halo = send(edge, edge_ext.at[:, 0:rows], h_send.at[2], h_recv.at[2], at(dlon=1))
    diag_halo = send(edge, edge_ext.at[:, rows:2 * rows], h_send.at[3], h_recv.at[3], at(dlat=-1, dlon=1))
    halos = [lat_halo, reg_halo, near_halo, diag_halo]

    def masks(ref, k):
        for i in range(rows):
            ids[i * levels:(i + 1) * levels, :] = ref[i].astype(jnp.float32)
        table = ids[...].astype(jnp.bfloat16)
        pos = lax.broadcasted_iota(jnp.int32, (levels * rows, win), 1)
        which = lax.broadcasted_iota(jnp.int32, (levels * rows, win), 0)
        pos_t = lax.broadcasted_iota(jnp.int32, (win, levels * rows), 0)
        which_t = lax.broadcasted_iota(jnp.int32, (win, levels * rows), 1)
        col = (lax.broadcasted_iota(jnp.int32, (cols, win), 0)
               == k * WLON + lax.broadcasted_iota(jnp.int32, (cols, win), 1) % WLON)
        col_t = (lax.broadcasted_iota(jnp.int32, (win, cols), 1)
                 == k * WLON + lax.broadcasted_iota(jnp.int32, (win, cols), 0) % WLON)
        wide = jnp.dot(table, col.astype(jnp.float32).astype(jnp.bfloat16), preferred_element_type=jnp.float32)
        tall = lax.dot_general(
            col_t.astype(jnp.float32).astype(jnp.bfloat16), table, (((1,), (1,)), ((), ())),
            preferred_element_type=jnp.float32)

        def row_of(p, lw):
            return (lw * WLAT + p % (WLAT * WLON) // WLON) * levels + p // (WLAT * WLON)

        for lw in range(rows // WLAT):
            r = jnp.sum(jnp.where(which == row_of(pos, lw), wide, 0.0), 0, keepdims=True)
            c = jnp.sum(jnp.where(which_t == row_of(pos_t, lw), tall, 0.0), 1, keepdims=True)
            mask[lw * 2 + 1 - k] = (r == c).astype(jnp.float32)

    def norm(lw):
        src = own if lw == 0 else ext
        for l in range(levels):
            for ii in range(WLAT):
                x = normalise(src[l, ii + shift].astype(jnp.float32))
                e = normalise(edge_ext[l, lw * WLAT + ii + shift])
                base = lw * 2 * win + l * WLAT * WLON + ii * WLON
                xw[base:base + 1, :] = e
                xw[base + 1:base + WLON, :] = x[0:WLON - 1]
                xw[base + win:base + win + WLON, :] = x[WLON - 1:2 * WLON - 1]
        for w in range(2 * lw, 2 * lw + 2):
            xn[w * win:(w + 1) * win, :] = xw[w * win:(w + 1) * win, :].astype(jnp.bfloat16)

    masks(reg_ref, 0)
    relay(0)
    reg_halo.wait_recv()
    masks(reg_prev, 1)
    near_halo.wait_recv()
    diag_halo.wait_recv()
    norm(0)
    relay(1)
    nwin = (rows // WLAT) * (cols // WLON)
    for w in range(nwin):
        xn[w * win:(w + 1) * win, :] = xw[w * win:(w + 1) * win, :].astype(jnp.bfloat16)

    lane = lax.broadcasted_iota(jnp.int32, (win, 128), 1)
    ones = jnp.ones((win, 128), jnp.bfloat16)
    hs = width // HEADS

    def attention(g, lw):
        both = slice(lw * 2 * win, (lw + 1) * 2 * win)
        for t in range(3):
            part = jnp.dot(
                xn[both, :], wqkv[g, :, t * gw:(t + 1) * gw], preferred_element_type=jnp.float32
            ).astype(jnp.bfloat16)
            for w in range(2):
                qkv[w, :, t * gw:(t + 1) * gw] = part[w * win:(w + 1) * win]

        def window(w, carry):
            allowed = mask[lw * 2 + w] > 0.5
            for pair in range(gw // 128):
                q = qkv[w, :, pair * 128:(pair + 1) * 128]
                k = qkv[w, :, gw + pair * 128:gw + (pair + 1) * 128]
                v = qkv[w, :, 2 * gw + pair * 128:2 * gw + (pair + 1) * 128]
                vones = jnp.concatenate([v, ones], axis=1)
                outs = []
                for h in range(128 // hs):
                    keep = (lane // hs == h).astype(jnp.float32) * (hs ** -0.5)
                    qh = (q.astype(jnp.float32) * keep).astype(jnp.bfloat16)
                    s = lax.dot_general(
                        qh, k, (((1,), (1,)), ((), ())), preferred_element_type=jnp.float32
                    )
                    s = jnp.where(allowed, s, -1e30)
                    e = jnp.exp(s - jnp.max(s, -1, keepdims=True)).astype(jnp.bfloat16)
                    o = jnp.dot(e, vones, preferred_element_type=jnp.float32)
                    outs.append(o[:, :128] / o[:, 128:])
                ow[w, :, pair * 128:(pair + 1) * 128] = jnp.where(lane < hs, outs[0], outs[1])
            return carry

        for w in range(2):
            window(w, 0)
        for l in range(levels):
            for ii in range(WLAT):
                i = lw * WLAT + ii
                r = l * WLAT * WLON + ii * WLON
                w = 0
                ret[g, l, i] = ow[w, r:r + 1, :].astype(jnp.bfloat16).astype(jnp.float32)
                nat[l, i, 0:WLON - 1, :] = ow[w, r + 1:r + WLON, :]
                nat[l, i, WLON - 1:2 * WLON - 1, :] = ow[w + 1, r:r + WLON, :]
                attn[g][l, HALO + i] = nat[l, i].astype(jnp.bfloat16)
    def give_rows(g):
        return [
            send(attn[g].at[:, rows:rows + HALO], attn[g].at[:, 0:HALO],
                 r_send.at[3 * g], r_recv.at[3 * g], at(dlat=1)),
        ]

    def give_edges(g):
        return [
            send(ret.at[g], ret_ext[g].at[:, rows:2 * rows],
                 r_send.at[3 * g + 1], r_recv.at[3 * g + 1], at(dlon=-1)),
            send(ret.at[g], ret_ext[g].at[:, 0:rows],
                 r_send.at[3 * g + 2], r_recv.at[3 * g + 2], at(dlat=1, dlon=-1)),
        ]

    nat[:, :, cols - 1:cols, :] = jnp.zeros((levels, rows, 1, gw), jnp.float32)
    row_id = lax.broadcasted_iota(jnp.int32, (cols, gw), 0)
    backs = []

    def gather(g):
        for c in backs[g]:
            c.wait_recv()
        for l in range(levels):
            for i in range(rows):
                a = attn[g][l, HALO + i - shift].astype(jnp.float32)
                e = ret_ext[g][l, rows + i - shift]
                r = (l * rows + i) * cols
                ymat[r:r + cols, g * gw:(g + 1) * gw] = jnp.where(row_id == cols - 1, e, a)

    finish(0)
    attention(0, 0)
    low_load.wait()
    lat_halo.wait_recv()
    norm(1)
    for g in range(GROUPS):
        if g > 0:
            finish(g)
        attention(g, 1)
        back = give_rows(g)
        relay(g + 2)
        if g > 0:
            attention(g, 0)
        backs.append(back + give_edges(g))
        if g > 0:
            gather(g - 1)
    finish(GROUPS)
    finish(GROUPS + 1)
    gather(GROUPS - 1)

    for l in range(levels):
        for j in range(rows // WLAT):
            r = (l * rows + j * WLAT) * cols
            y = ymat[r:r + WLAT * cols, :].astype(jnp.bfloat16)
            here = slice(j * WLAT, (j + 1) * WLAT)
            for n in range(OUTS):
                side_cols = slice(n * owid, (n + 1) * owid)
                p = jnp.dot(y, wout[n], preferred_element_type=jnp.float32)
                t = own[l, here, :, side_cols].astype(jnp.float32)
                out_ref[l, here, :, side_cols] = (t + p.reshape(t.shape)).astype(jnp.bfloat16)

    for c in sent + halos + sum(backs, []):
        c.wait_send()


def local(sizes, tokens, weights, regions, offsets):
    block = tokens[0]
    levels, rows, cols, width = block.shape
    win = WLEV * WLAT * WLON
    nwin = (rows // WLAT) * (cols // WLON)
    gw = width // GROUPS
    nw = (GROUPS + OUTS) * (1 + 4 * (sizes[0] // 2 - 1))
    bf, f32 = jnp.bfloat16, jnp.float32
    dma = pltpu.SemaphoreType.DMA
    anywhere = pl.BlockSpec(memory_space=pl.ANY)
    out = pl.pallas_call(
        functools.partial(kernel, sizes),
        out_shape=jax.ShapeDtypeStruct(block.shape, bf),
        in_specs=[pl.BlockSpec(memory_space=pltpu.SMEM), anywhere, anywhere, pl.BlockSpec(memory_space=pltpu.VMEM)],
        out_specs=pl.BlockSpec(memory_space=pltpu.VMEM),
        scratch_shapes=[
            pltpu.VMEM((GROUPS, width, 3 * gw), bf),
            pltpu.VMEM((OUTS, width, width // OUTS), bf),
            pltpu.VMEM((levels, rows, cols, width), bf),
            pltpu.VMEM((levels, rows - WLAT + HALO, cols, width), bf),
            pltpu.VMEM((levels, rows, 1, width), f32),
            pltpu.VMEM((levels, 2 * rows, 1, width), f32),
            pltpu.VMEM((rows, levels, cols), jnp.int32),
            pltpu.VMEM((levels * rows, cols), f32),
            pltpu.VMEM((nwin, win, win), f32),
            pltpu.VMEM((nwin * win, width), f32),
            pltpu.VMEM((nwin * win, width), bf),
            pltpu.VMEM((2, win, 3 * gw), bf),
            pltpu.VMEM((2, win, gw), f32),
            pltpu.VMEM((levels, rows, cols, gw), f32),
            pltpu.VMEM((GROUPS, levels, rows, 1, gw), f32),
            pltpu.VMEM((levels * rows * cols, width), f32),
            dma((3 * GROUPS + OUTS + 2,)),
            dma((nw,)),
            dma((nw,)),
            dma((4,)),
            dma((4,)),
            dma((3 * GROUPS,)),
            dma((3 * GROUPS,)),
        ]
        + [pltpu.VMEM((levels, rows + HALO, cols, gw), bf)] * GROUPS
        + [pltpu.VMEM((levels, 2 * rows, 1, gw), f32)] * GROUPS,
        compiler_params=pltpu.CompilerParams(
            collective_id=0, has_side_effects=True, vmem_limit_bytes=56 * 1024 * 1024
        ),
    )(offsets, block, weights, regions.transpose(1, 0, 2))
    return out[None]


def solution(mesh):
    sizes = (mesh.shape["batch"], mesh.shape["lat"], mesh.shape["lon"])
    in_specs = (P("batch", None, "lat", "lon", None), P("batch", None), P(None, "lat", "lon"), P())
    out_specs = P("batch", None, "lat", "lon", None)
    return jax.shard_map(
        functools.partial(local, sizes), mesh=mesh, in_specs=in_specs, out_specs=out_specs, check_vma=False
    )
```
